32 devices in a mesh: grp: 8 (over z, core), swap: 4 (over y, x).
Axes of the slice: x: 2, y: 2, z: 4, core: 2. Of those that a mesh axis runs over, the one named last changes fastest.
Arguments:
- amplitudes: float32 [2, 8, 4, 4, 4, 8, 8, 128], P(None, 'grp', 'swap'), may hold values from -6 to 6
- low_gates: float32 [3, 2, 128, 128], replicated, may hold values from -0.375 to 0.375
- mid_gates: float32 [2, 2, 128, 128], replicated, may hold values from -0.375 to 0.375
- pair_gate: float32 [2, 2, 2], replicated, may hold values from -3 to 3
- slice_bits: int32 [13], replicated, may hold values from 0 to 1
- phase_angles: float32 [13, 128], replicated, may hold values from -3.140625 to 3.140625
Outputs:
- final_state: float32 [2, 8, 4, 4, 4, 8, 8, 128], P(None, 'grp', 'swap')
The draws below stay inside these ranges and needn't reach their ends.
All inputs are finite; a program needn't handle non-finite values.
Results may differ from the reference program's by a relative error of at most 0.00007.
Values sent between devices are 32-bit elements; how exact they have to be, the bound alone decides.
A program may use at most 64 MiB of HBM per device.

```python
import jax
import jax.numpy as jnp
from jax import lax

FIXED = 13
LOW = 128
TRADE = 16
MIDQ = 8
ROWS = 8
NG = 8
NS = 4
PB = 4


def plant(values, rng, low, top_value):
    spot = [jax.random.randint(jax.random.fold_in(rng, axis), (), 0, length) for axis, length in enumerate(values.shape)]
    longest = values.shape.index(max(values.shape))
    next_to = spot[:longest] + [(spot[longest] + 1) % values.shape[longest]] + spot[longest + 1:]
    return values.at[tuple(spot)].set(low).at[tuple(next_to)].set(top_value)


def block_scale(key, extent, shards, least, largest):
    def one(axis_at, shards_of):
        steps = jax.random.uniform(jax.random.fold_in(jax.random.fold_in(key, 6), axis_at), (shards_of,), jnp.float32, least / len(shards), largest / len(shards))
        return jnp.repeat(jnp.exp(steps), extent[axis_at] // shards_of).reshape((-1,) + (1,) * (len(extent) - axis_at - 1))

    factor_of = one(*shards[0])
    for cut in shards[1:]:
        factor_of = factor_of * one(*cut)
    return factor_of


def noise(key, extent, spread, reach, cuts=(), held_as=jnp.bfloat16):
    values = spread * jax.random.normal(key, extent, jnp.float32)
    if cuts:
        values = values * block_scale(key, extent, cuts, -0.22, 0.18)
    return jnp.clip(values, -reach, reach).astype(held_as)


def setup_inputs(seed: int = 0) -> dict:
    keys = jax.random.split(jax.random.key(seed), 7)
    amplitudes = noise(keys[0], (2, NG, NS, NS, PB, MIDQ, ROWS, LOW), 1.0, 6.0, ((1, 8), (2, 4)), jnp.float32)
    low_gates = noise(keys[1], (3, 2, LOW, LOW), (2 * LOW) ** -0.5, 0.375, (), jnp.float32)
    mid_gates = noise(keys[2], (2, 2, TRADE * MIDQ, TRADE * MIDQ), (2 * TRADE * MIDQ) ** -0.5, 0.375, (), jnp.float32)
    pair_gate = noise(keys[3], (2, 2, 2), 4 ** -0.5, 3.0, (), jnp.float32)
    slice_bits = plant(jax.random.randint(keys[4], (FIXED,), 0, 2), jax.random.fold_in(keys[4], 1), 0, 1).astype(jnp.int32)
    phase_angles = jnp.clip(jax.random.uniform(keys[5], (FIXED, LOW), jnp.float32, -3.140625, 3.140625), -3.140625, 3.140625)
    return {"amplitudes": amplitudes, "low_gates": low_gates, "mid_gates": mid_gates, "pair_gate": pair_gate, "slice_bits": slice_bits, "phase_angles": phase_angles}


highest = lax.Precision.HIGHEST


def low_gate(psi, matrix):
    real_part = jnp.einsum("...k,ik->...i", psi[0], matrix[0], precision=highest, preferred_element_type=jnp.float32) - jnp.einsum("...k,ik->...i", psi[1], matrix[1], precision=highest, preferred_element_type=jnp.float32)
    imag_part = jnp.einsum("...k,ik->...i", psi[1], matrix[0], precision=highest, preferred_element_type=jnp.float32) + jnp.einsum("...k,ik->...i", psi[0], matrix[1], precision=highest, preferred_element_type=jnp.float32)
    return jnp.stack([real_part, imag_part])


def mid_gate(psi, matrix):
    shape_now = psi.shape
    order = matrix.shape[1]
    flat = psi.reshape(2, -1, order, shape_now[-2] * shape_now[-1])
    real_part = jnp.einsum("ik,bkm->bim", matrix[0], flat[0], precision=highest, preferred_element_type=jnp.float32) - jnp.einsum("ik,bkm->bim", matrix[1], flat[1], precision=highest, preferred_element_type=jnp.float32)
    imag_part = jnp.einsum("ik,bkm->bim", matrix[0], flat[1], precision=highest, preferred_element_type=jnp.float32) + jnp.einsum("ik,bkm->bim", matrix[1], flat[0], precision=highest, preferred_element_type=jnp.float32)
    return jnp.stack([real_part, imag_part]).reshape(shape_now)


def reference(amplitudes, low_gates, mid_gates, pair_gate, slice_bits, phase_angles):
    theta = jnp.dot(slice_bits.astype(jnp.float32), phase_angles, precision=highest, preferred_element_type=jnp.float32)
    cosine = jnp.cos(theta)
    sine = jnp.sin(theta)
    phased = jnp.stack([amplitudes[0] * cosine - amplitudes[1] * sine, amplitudes[0] * sine + amplitudes[1] * cosine])
    first = low_gate(phased, low_gates[0])
    second = mid_gate(first, mid_gates[0])
    third = low_gate(second, low_gates[1])
    outer = third.shape[1]
    halves = third.reshape((2, 2, outer // 2) + third.shape[2:])
    lower = halves[:, 0]
    upper = halves[:, 1]

    def pair_row(target):
        real_part = (pair_gate[0, target, 0] * lower[0] - pair_gate[1, target, 0] * lower[1]) + (pair_gate[0, target, 1] * upper[0] - pair_gate[1, target, 1] * upper[1])
        imag_part = (pair_gate[0, target, 0] * lower[1] + pair_gate[1, target, 0] * lower[0]) + (pair_gate[0, target, 1] * upper[1] + pair_gate[1, target, 1] * upper[0])
        return jnp.stack([real_part, imag_part])

    paired = jnp.stack([pair_row(0), pair_row(1)], axis=1).reshape(third.shape)
    traded = jnp.swapaxes(paired, 2, 3)
    fourth = mid_gate(traded, mid_gates[1])
    return low_gate(fourth, low_gates[2])
```

```python
import functools

import jax
import jax.numpy as jnp
from jax import lax
from jax.experimental import pallas as pl
from jax.experimental.pallas import tpu as pltpu
from jax.sharding import PartitionSpec as P

MESH = pl.DeviceIdType.MESH
highest = lax.Precision.HIGHEST


def dot(a, b):
    return jnp.dot(a, b, precision=highest, preferred_element_type=jnp.float32)


def dot_nt(a, b):
    return lax.dot_general(
        a, b, (((1,), (1,)), ((), ())), precision=highest, preferred_element_type=jnp.float32
    )


def embedded(re, im):
    return jnp.concatenate(
        [jnp.concatenate([re, -im], axis=1), jnp.concatenate([im, re], axis=1)], axis=0
    )


def mixed(own, other, own_re, own_im, other_re, other_im):
    re = (own[0] * own_re - own[1] * own_im) + (other[0] * other_re - other[1] * other_im)
    im = (own[0] * own_im + own[1] * own_re) + (other[0] * other_im + other[1] * other_re)
    return re, im


def kernel(
    dims,
    x_ref, half_ref, low_ref, mid_ref, pair_in, bits_in, angle_ref,
    out_v,
    x_v, low_v, mid_v, angle_v, pair_ref, bits_ref,
    early_rx, early_y, early_t, late_y, late_t, late_z, late_rz,
    load_sem, ze_send, ze_recv, zl_send, zl_recv, ae_send, ae_recv, al_send, al_recv,
    passing, stash, hop_sem, onward_sem, stash_sem, after_sem, near_sem, all_sem,
):
    groups, swaps, m_size, rows, low, early, blocks, pieces, lead, kept = dims
    late = rows - early
    part = m_size // swaps
    piece = m_size // blocks
    grp = lax.axis_index("grp")
    me = lax.axis_index("swap")
    half = groups // 2
    quarter = groups // 4
    top = grp // half
    layer = grp // quarter
    partner = (grp + half) % groups

    def on(*layers):
        hit = layer == layers[0]
        for other in layers[1:]:
            hit = jnp.logical_or(hit, layer == other)
        return pl.when(hit)

    def tell(sem, to):
        pl.semaphore_signal(sem, inc=1, device_id={"grp": to}, device_id_type=MESH)

    def tell_peers(sem):
        for d in range(1, swaps):
            pl.semaphore_signal(
                sem, inc=1, device_id={"swap": lax.bitwise_xor(me, d)}, device_id_type=MESH
            )

    barrier = pltpu.get_barrier_semaphore()

    @on(2)
    def _():
        tell(barrier, grp - quarter)
        tell(barrier, grp - half)
        tell(barrier, grp + quarter)

    @on(0)
    def _():
        tell(barrier, grp + half)
        tell(barrier, grp + half + quarter)

    @on(1)
    def _():
        tell(barrier, grp + half)

    @on(3)
    def _():
        tell_peers(barrier)

    span = m_size // pieces

    def x_row(c, r):
        return x_v[pl.ds(c * m_size * rows + r, m_size, stride=rows), :]

    raw, hop, onward = [], [], []
    for j in range(pieces):
        at = pl.ds(j * span, span)
        raw.append(
            pltpu.make_async_remote_copy(
                src_ref=half_ref.at[:, at, 0], dst_ref=early_rx.at[:, at],
                send_sem=ze_send.at[j], recv_sem=ze_recv.at[j],
                device_id={"grp": partner}, device_id_type=MESH,
            )
        )
        if j < lead:
            hop.append(
                pltpu.make_async_remote_copy(
                    src_ref=half_ref.at[:, at, 0], dst_ref=passing.at[:, at],
                    send_sem=ze_send.at[j], recv_sem=hop_sem.at[j],
                    device_id={"grp": (grp + quarter) % groups}, device_id_type=MESH,
                )
            )
            onward.append(
                pltpu.make_async_remote_copy(
                    src_ref=passing.at[:, at], dst_ref=early_rx.at[:, at],
                    send_sem=onward_sem.at[j], recv_sem=ze_recv.at[j],
                    device_id={"grp": (grp + quarter) % groups}, device_id_type=MESH,
                )
            )

    @on(0, 1, 2)
    def _():
        pl.semaphore_wait(barrier, 1)

    @on(3)
    def _():
        pl.semaphore_wait(barrier, swaps + 2)
        tell_peers(near_sem)

    for j in range(pieces):
        on(0, 2, 3)(raw[j].start)
        if j < lead:
            on(1)(hop[j].start)
    loads = [
        pltpu.make_async_copy(src, dst, load_sem.at[i])
        for i, (src, dst) in enumerate(
            [(bits_in, bits_ref), (angle_ref, angle_v), (low_ref, low_v), (mid_ref, mid_v), (pair_in, pair_ref), (x_ref, x_v)]
        )
    ]
    for load in loads:
        load.start()

    @on(3)
    def _():
        pl.semaphore_wait(near_sem, swaps - 1)
        for back in range(1, 4):
            tell(all_sem, grp - back * quarter)

    for load in loads:
        load.wait()
    theta = bits_ref[0].astype(jnp.float32) * angle_v[0:1, :]
    for j in range(1, angle_v.shape[0]):
        theta = theta + bits_ref[j].astype(jnp.float32) * angle_v[j : j + 1, :]
    cosine, sine = jnp.cos(theta), jnp.sin(theta)
    w = jnp.concatenate([low_v[0, 0], low_v[0, 1]], axis=0)
    for i in range(1, low_v.shape[0]):
        w = dot(embedded(low_v[i, 0], low_v[i, 1]), w)
    w_re, w_im = w[:low], w[low:]
    w = embedded(w_re * cosine - w_im * sine, w_re * sine + w_im * cosine)

    @on(0, 1, 2)
    def _():
        pl.semaphore_wait(all_sem, 1)

    for j in range(lead, pieces):
        on(1)(raw[j].start)
    mid_first = embedded(mid_v[0, 0], mid_v[0, 1])
    mid_second = embedded(mid_v[1, 0], mid_v[1, 1])

    def first_gates(pairs, y_ref):
        for i, (re, im) in enumerate(pairs):
            y = dot_nt(jnp.concatenate([re, im], axis=1), w)
            y = dot(mid_first, jnp.concatenate([y[:, :low], y[:, low:]], axis=0))
            y_ref[i, 0] = y[:m_size]
            y_ref[i, 1] = y[m_size:]

    def trade(y_ref, t_ref, send, recv):
        mine = pl.ds(pl.multiple_of(me * part, part), part)
        copies = []
        for d in range(1, swaps):
            to = lax.bitwise_xor(me, d)
            copy = pltpu.make_async_remote_copy(
                src_ref=y_ref.at[:, :, pl.ds(pl.multiple_of(to * part, part), part), :],
                dst_ref=t_ref.at[:, :, mine, :],
                send_sem=send.at[d], recv_sem=recv.at[d],
                device_id={"swap": to}, device_id_type=MESH,
            )
            copy.start()
            copies.append(copy)
        t_ref[:, :, mine, :] = y_ref[:, :, mine, :]
        for copy in copies:
            copy.wait()

    def last_gate(t_ref, i):
        z = dot(mid_second, jnp.concatenate([t_ref[i, 0], t_ref[i, 1]], axis=0))
        return z[:m_size], z[m_size:]

    own_re, own_im = pair_ref[0, top, top], pair_ref[1, top, top]
    other_re, other_im = pair_ref[0, top, 1 - top], pair_ref[1, top, 1 - top]

    first_gates([(x_row(0, r), x_row(1, r)) for r in range(early, rows)], late_y)
    for j in range(lead):
        on(2)(hop[j].wait_recv)
        on(2)(onward[j].start)
    trade(late_y, late_t, al_send, al_recv)
    for i in range(late):
        z_re, z_im = last_gate(late_t, i)
        late_z[i, 0] = z_re
        late_z[i, 1] = z_im
    finished, aside, after = [], [], []
    for k in range(blocks):
        rows_k = pl.ds(k * piece, piece)
        finished.append(
            pltpu.make_async_remote_copy(
                src_ref=late_z.at[:, :, rows_k, :], dst_ref=late_rz.at[:, :, rows_k, :],
                send_sem=zl_send.at[k], recv_sem=zl_recv.at[k],
                device_id={"grp": partner}, device_id_type=MESH,
            )
        )
        if k >= blocks - kept:
            h = k - (blocks - kept)
            rows_h = pl.ds(h * piece, piece)
            aside.append(
                pltpu.make_async_remote_copy(
                    src_ref=late_z.at[:, :, rows_k, :], dst_ref=stash.at[:, :, rows_h, :],
                    send_sem=zl_send.at[k], recv_sem=stash_sem.at[h],
                    device_id={"grp": (grp + 3 * quarter) % groups}, device_id_type=MESH,
                )
            )
            after.append(
                pltpu.make_async_remote_copy(
                    src_ref=stash.at[:, :, rows_h, :], dst_ref=late_rz.at[:, :, rows_k, :],
                    send_sem=after_sem.at[h], recv_sem=zl_recv.at[k],
                    device_id={"grp": (grp + 3 * quarter) % groups}, device_id_type=MESH,
                )
            )

    @on(1)
    def _():
        for copy in finished:
            copy.start()

    @on(2)
    def _():
        for copy in finished:
            copy.start()
        for h in range(kept):
            aside[h].wait_recv()
            after[h].start()

    @on(3)
    def _():
        for copy in aside:
            copy.start()

    for copy in raw:
        copy.wait()

    @on(0)
    def _():
        for copy in finished:
            copy.start()

    @on(3)
    def _():
        for copy in finished[: blocks - kept]:
            copy.start()

    first_gates(
        [
            mixed(
                (x_row(0, r), x_row(1, r)), (early_rx[0, :, r, :], early_rx[1, :, r, :]),
                own_re, own_im, other_re, other_im,
            )
            for r in range(early)
        ],
        early_y,
    )
    trade(early_y, early_t, ae_send, ae_recv)
    for r in range(early):
        for c, value in enumerate(last_gate(early_t, r)):
            out_v[pl.ds(c * m_size * rows + r, m_size, stride=rows), :] = value

    for k in range(blocks):
        finished[k].wait_recv()
        at = slice(k * piece, (k + 1) * piece)
        for i in range(late):
            pair = mixed(
                (late_z[i, 0, at], late_z[i, 1, at]), (late_rz[i, 0, at], late_rz[i, 1, at]),
                own_re, own_im, other_re, other_im,
            )
            for c in range(2):
                start = (c * m_size + k * piece) * rows + early + i
                out_v[pl.ds(start, piece, stride=rows), :] = pair[c]
    for copy in finished:
        copy.wait_send()
    for copy in after:
        on(2)(copy.wait_send)
    for copy in onward:
        on(2)(copy.wait_send)


def local(groups, swaps, amplitudes, low_gates, mid_gates, pair_gate, slice_bits, phase_angles):
    _, _, _, a_size, b_size, q_size, rows, low = amplitudes.shape
    m_size = a_size * b_size * q_size
    early = rows // 2
    late = rows - early
    blocks, pieces, lead, kept = 8, 8, 1, 2
    flat = amplitudes.reshape(2 * m_size * rows, low)
    halves = amplitudes.reshape(2, m_size, 2, early, low)
    f32 = jnp.float32
    dma = pltpu.SemaphoreType.DMA
    anywhere = pl.BlockSpec(memory_space=pl.ANY)
    in_hbm = [
        pltpu.with_memory_space_constraint(value, pltpu.HBM)
        for value in (flat, halves, low_gates, mid_gates, pair_gate, slice_bits, phase_angles)
    ]
    out = pl.pallas_call(
        functools.partial(kernel, (groups, swaps, m_size, rows, low, early, blocks, pieces, lead, kept)),
        out_shape=pltpu.VMEM(flat.shape, f32),
        in_specs=[anywhere] * 7,
        out_specs=pl.BlockSpec(memory_space=pltpu.VMEM),
        scratch_shapes=[
            pltpu.VMEM(flat.shape, f32),
            pltpu.VMEM(low_gates.shape, f32),
            pltpu.VMEM(mid_gates.shape, f32),
            pltpu.VMEM(phase_angles.shape, f32),
            pltpu.SMEM(pair_gate.shape, f32),
            pltpu.SMEM(slice_bits.shape, jnp.int32),
        ]
        + [pltpu.VMEM((2, m_size, early, low), f32)]
        + [pltpu.VMEM((early, 2, m_size, low), f32)] * 2
        + [pltpu.VMEM((late, 2, m_size, low), f32)] * 4
        + [
            dma((6,)),
            dma((pieces,)), dma((pieces,)),
            dma((blocks,)), dma((blocks,)),
            dma((swaps,)), dma((swaps,)), dma((swaps,)), dma((swaps,)),
            pltpu.VMEM((2, lead * m_size // pieces, early, low), f32),
            pltpu.VMEM((late, 2, kept * m_size // blocks, low), f32),
            dma((lead,)), dma((lead,)), dma((kept,)), dma((kept,)),
            pltpu.SemaphoreType.REGULAR, pltpu.SemaphoreType.REGULAR,
        ],
        compiler_params=pltpu.CompilerParams(
            collective_id=0, has_side_effects=True, vmem_limit_bytes=24 << 20
        ),
        name="evolve",
    )(*in_hbm)
    return out.reshape(amplitudes.shape)


def solution(mesh):
    spec = P(None, "grp", "swap", None, None, None, None, None)
    return jax.shard_map(
        functools.partial(local, mesh.shape["grp"], mesh.shape["swap"]),
        mesh=mesh,
        in_specs=(spec, P(), P(), P(), P(), P()),
        out_specs=spec,
        check_vma=False,
    )
```

```python
import functools

import jax
import jax.numpy as jnp
from jax import lax
from jax.experimental import pallas as pl
from jax.experimental.pallas import tpu as pltpu
from jax.sharding import PartitionSpec as P

MESH = pl.DeviceIdType.MESH
highest = lax.Precision.HIGHEST


def dot(a, b):
    return jnp.dot(a, b, precision=highest, preferred_element_type=jnp.float32)


def dot_nt(a, b):
    return lax.dot_general(
        a, b, (((1,), (1,)), ((), ())), precision=highest, preferred_element_type=jnp.float32
    )


def embedded(re, im):
    return jnp.concatenate(
        [jnp.concatenate([re, -im], axis=1), jnp.concatenate([im, re], axis=1)], axis=0
    )


def mixed(own, other, own_re, own_im, other_re, other_im):
    re = (own[0] * own_re - own[1] * own_im) + (other[0] * other_re - other[1] * other_im)
    im = (own[0] * own_im + own[1] * own_re) + (other[0] * other_im + other[1] * other_re)
    return re, im


def kernel(
    dims,
    x_ref, half_ref, low_ref, mid_ref, pair_in, bits_in, angle_ref,
    out_v,
    x_v, low_v, mid_v, angle_v, pair_ref, bits_ref,
    early_rx, early_y, early_t, late_y, late_t, late_z, late_rz,
    load_sem, ze_send, ze_recv, zl_send, zl_recv, ae_send, ae_recv, al_send, al_recv,
    passing, stash, hop_sem, onward_sem, stash_sem, after_sem, near_sem, all_sem,
):
    groups, swaps, m_size, rows, low, early, blocks, pieces, lead, kept = dims
    late = rows - early
    part = m_size // swaps
    piece = m_size // blocks
    grp = lax.axis_index("grp")
    me = lax.axis_index("swap")
    half = groups // 2
    quarter = groups // 4
    top = grp // half
    layer = grp // quarter
    partner = (grp + half) % groups

    def on(*layers):
        hit = layer == layers[0]
        for other in layers[1:]:
            hit = jnp.logical_or(hit, layer == other)
        return pl.when(hit)

    def tell(sem, to):
        pl.semaphore_signal(sem, inc=1, device_id={"grp": to}, device_id_type=MESH)

    def tell_peers(sem):
        for d in range(1, swaps):
            pl.semaphore_signal(
                sem, inc=1, device_id={"swap": lax.bitwise_xor(me, d)}, device_id_type=MESH
            )

    barrier = pltpu.get_barrier_semaphore()

    @on(2)
    def _():
        tell(barrier, grp - quarter)
        tell(barrier, grp - half)
        tell(barrier, grp + quarter)

    @on(0)
    def _():
        tell(barrier, grp + half)
        tell(barrier, grp + half + quarter)

    @on(1)
    def _():
        tell(barrier, grp + half)

    @on(3)
    def _():
        tell_peers(barrier)

    span = m_size // pieces

    def x_row(c, r):
        return x_v[pl.ds(c * m_size * rows + r, m_size, stride=rows), :]

    raw, hop, onward = [], [], []
    for j in range(pieces):
        at = pl.ds(j * span, span)
        raw.append(
            pltpu.make_async_remote_copy(
                src_ref=half_ref.at[:, at, 0], dst_ref=early_rx.at[:, at],
                send_sem=ze_send.at[j], recv_sem=ze_recv.at[j],
                device_id={"grp": partner}, device_id_type=MESH,
            )
        )
        if j < lead:
            hop.append(
                pltpu.make_async_remote_copy(
                    src_ref=half_ref.at[:, at, 0], dst_ref=passing.at[:, at],
                    send_sem=ze_send.at[j], recv_sem=hop_sem.at[j],
                    device_id={"grp": (grp + quarter) % groups}, device_id_type=MESH,
                )
            )
            onward.append(
                pltpu.make_async_remote_copy(
                    src_ref=passing.at[:, at], dst_ref=early_rx.at[:, at],
                    send_sem=onward_sem.at[j], recv_sem=ze_recv.at[j],
                    device_id={"grp": (grp + quarter) % groups}, device_id_type=MESH,
                )
            )

    @on(0, 1, 2)
    def _():
        pl.semaphore_wait(barrier, 1)

    @on(3)
    def _():
        pl.semaphore_wait(barrier, swaps + 2)
        tell_peers(near_sem)

    for j in range(pieces):
        on(0, 2, 3)(raw[j].start)
        if j < lead:
            on(1)(hop[j].start)
    loads = [
        pltpu.make_async_copy(src, dst, load_sem.at[i])
        for i, (src, dst) in enumerate(
            [(bits_in, bits_ref), (angle_ref, angle_v), (low_ref, low_v), (mid_ref, mid_v), (pair_in, pair_ref), (x_ref, x_v)]
        )
    ]
    for load in loads:
        load.start()

    @on(3)
    def _():
        pl.semaphore_wait(near_sem, swaps - 1)
        for back in range(1, 4):
            tell(all_sem, grp - back * quarter)

    for load in loads:
        load.wait()
    theta = bits_ref[0].astype(jnp.float32) * angle_v[0:1, :]
    for j in range(1, angle_v.shape[0]):
        theta = theta + bits_ref[j].astype(jnp.float32) * angle_v[j : j + 1, :]
    cosine, sine = jnp.cos(theta), jnp.sin(theta)
    w = jnp.concatenate([low_v[0, 0], low_v[0, 1]], axis=0)
    for i in range(1, low_v.shape[0]):
        w = dot(embedded(low_v[i, 0], low_v[i, 1]), w)
    w_re, w_im = w[:low], w[low:]
    w = embedded(w_re * cosine - w_im * sine, w_re * sine + w_im * cosine)

    @on(0, 1, 2)
    def _():
        pl.semaphore_wait(all_sem, 1)

    for j in range(lead, pieces):
        on(1)(raw[j].start)
    mid_first = embedded(mid_v[0, 0], mid_v[0, 1])
    mid_second = embedded(mid_v[1, 0], mid_v[1, 1])

    def first_gates(pairs, y_ref):
        for i, (re, im) in enumerate(pairs):
            y = dot_nt(jnp.concatenate([re, im], axis=1), w)
            y = dot(mid_first, jnp.concatenate([y[:, :low], y[:, low:]], axis=0))
            y_ref[i, 0] = y[:m_size]
            y_ref[i, 1] = y[m_size:]

    def trade(y_ref, t_ref, send, recv):
        mine = pl.ds(pl.multiple_of(me * part, part), part)
        copies = []
        for d in range(1, swaps):
            to = lax.bitwise_xor(me, d)
            copy = pltpu.make_async_remote_copy(
                src_ref=y_ref.at[:, :, pl.ds(pl.multiple_of(to * part, part), part), :],
                dst_ref=t_ref.at[:, :, mine, :],
                send_sem=send.at[d], recv_sem=recv.at[d],
                device_id={"swap": to}, device_id_type=MESH,
            )
            copy.start()
            copies.append(copy)
        t_ref[:, :, mine, :] = y_ref[:, :, mine, :]
        for copy in copies:
            copy.wait()

    def last_gate(t_ref, i):
        z = dot(mid_second, jnp.concatenate([t_ref[i, 0], t_ref[i, 1]], axis=0))
        return z[:m_size], z[m_size:]

    own_re, own_im = pair_ref[0, top, top], pair_ref[1, top, top]
    other_re, other_im = pair_ref[0, top, 1 - top], pair_ref[1, top, 1 - top]

    first_gates([(x_row(0, r), x_row(1, r)) for r in range(early, rows)], late_y)
    for j in range(lead):
        on(2)(hop[j].wait_recv)
        on(2)(onward[j].start)
    trade(late_y, late_t, al_send, al_recv)
    for i in range(late):
        z_re, z_im = last_gate(late_t, i)
        late_z[i, 0] = z_re
        late_z[i, 1] = z_im
    finished, aside, after = [], [], []
    for k in range(blocks):
        rows_k = pl.ds(k * piece, piece)
        finished.append(
            pltpu.make_async_remote_copy(
                src_ref=late_z.at[:, :, rows_k, :], dst_ref=late_rz.at[:, :, rows_k, :],
                send_sem=zl_send.at[k], recv_sem=zl_recv.at[k],
                device_id={"grp": partner}, device_id_type=MESH,
            )
        )
        if k >= blocks - kept:
            h = k - (blocks - kept)
            rows_h = pl.ds(h * piece, piece)
            aside.append(
                pltpu.make_async_remote_copy(
                    src_ref=late_z.at[:, :, rows_k, :], dst_ref=stash.at[:, :, rows_h, :],
                    send_sem=zl_send.at[k], recv_sem=stash_sem.at[h],
                    device_id={"grp": (grp + 3 * quarter) % groups}, device_id_type=MESH,
                )
            )
            after.append(
                pltpu.make_async_remote_copy(
                    src_ref=stash.at[:, :, rows_h, :], dst_ref=late_rz.at[:, :, rows_k, :],
                    send_sem=after_sem.at[h], recv_sem=zl_recv.at[k],
                    device_id={"grp": (grp + 3 * quarter) % groups}, device_id_type=MESH,
                )
            )

    @on(1)
    def _():
        for copy in finished:
            copy.start()

    @on(2)
    def _():
        for copy in finished:
            copy.start()
        for h in range(kept):
            aside[h].wait_recv()
            after[h].start()

    @on(3)
    def _():
        for copy in aside:
            copy.start()
        for copy in finished[: blocks - kept]:
            copy.start()

    for copy in raw:
        copy.wait()

    @on(0)
    def _():
        for copy in finished:
            copy.start()

    first_gates(
        [
            mixed(
                (x_row(0, r), x_row(1, r)), (early_rx[0, :, r, :], early_rx[1, :, r, :]),
                own_re, own_im, other_re, other_im,
            )
            for r in range(early)
        ],
        early_y,
    )
    trade(early_y, early_t, ae_send, ae_recv)
    for r in range(early):
        for c, value in enumerate(last_gate(early_t, r)):
            out_v[pl.ds(c * m_size * rows + r, m_size, stride=rows), :] = value

    for k in range(blocks):
        if k == blocks - 1:
            for copy in finished:
                copy.wait_send()
            for copy in onward + after:
                on(2)(copy.wait_send)
        finished[k].wait_recv()
        at = slice(k * piece, (k + 1) * piece)
        for i in range(late):
            pair = mixed(
                (late_z[i, 0, at], late_z[i, 1, at]), (late_rz[i, 0, at], late_rz[i, 1, at]),
                own_re, own_im, other_re, other_im,
            )
            for c in range(2):
                start = (c * m_size + k * piece) * rows + early + i
                out_v[pl.ds(start, piece, stride=rows), :] = pair[c]


def local(groups, swaps, amplitudes, low_gates, mid_gates, pair_gate, slice_bits, phase_angles):
    _, _, _, a_size, b_size, q_size, rows, low = amplitudes.shape
    m_size = a_size * b_size * q_size
    early = rows // 2
    late = rows - early
    blocks, pieces, lead, kept = 8, 8, 2, 3
    flat = amplitudes.reshape(2 * m_size * rows, low)
    halves = amplitudes.reshape(2, m_size, 2, early, low)
    f32 = jnp.float32
    dma = pltpu.SemaphoreType.DMA
    anywhere = pl.BlockSpec(memory_space=pl.ANY)
    in_hbm = [
        pltpu.with_memory_space_constraint(value, pltpu.HBM)
        for value in (flat, halves, low_gates, mid_gates, pair_gate, slice_bits, phase_angles)
    ]
    out = pl.pallas_call(
        functools.partial(kernel, (groups, swaps, m_size, rows, low, early, blocks, pieces, lead, kept)),
        out_shape=pltpu.VMEM(flat.shape, f32),
        in_specs=[anywhere] * 7,
        out_specs=pl.BlockSpec(memory_space=pltpu.VMEM),
        scratch_shapes=[
            pltpu.VMEM(flat.shape, f32),
            pltpu.VMEM(low_gates.shape, f32),
            pltpu.VMEM(mid_gates.shape, f32),
            pltpu.VMEM(phase_angles.shape, f32),
            pltpu.SMEM(pair_gate.shape, f32),
            pltpu.SMEM(slice_bits.shape, jnp.int32),
        ]
        + [pltpu.VMEM((2, m_size, early, low), f32)]
        + [pltpu.VMEM((early, 2, m_size, low), f32)] * 2
        + [pltpu.VMEM((late, 2, m_size, low), f32)] * 4
        + [
            dma((6,)),
            dma((pieces,)), dma((pieces,)),
            dma((blocks,)), dma((blocks,)),
            dma((swaps,)), dma((swaps,)), dma((swaps,)), dma((swaps,)),
            pltpu.VMEM((2, lead * m_size // pieces, early, low), f32),
            pltpu.VMEM((late, 2, kept * m_size // blocks, low), f32),
            dma((lead,)), dma((lead,)), dma((kept,)), dma((kept,)),
            pltpu.SemaphoreType.REGULAR, pltpu.SemaphoreType.REGULAR,
        ],
        compiler_params=pltpu.CompilerParams(
            collective_id=0, has_side_effects=True, vmem_limit_bytes=24 << 20
        ),
        name="evolve",
    )(*in_hbm)
    return out.reshape(amplitudes.shape)


def solution(mesh):
    spec = P(None, "grp", "swap", None, None, None, None, None)
    return jax.shard_map(
        functools.partial(local, mesh.shape["grp"], mesh.shape["swap"]),
        mesh=mesh,
        in_specs=(spec, P(), P(), P(), P(), P()),
        out_specs=spec,
        check_vma=False,
    )
```

```python
import functools

import jax
import jax.numpy as jnp
from jax import lax
from jax.experimental import pallas as pl
from jax.experimental.pallas import tpu as pltpu
from jax.sharding import PartitionSpec as P

MESH = pl.DeviceIdType.MESH
highest = lax.Precision.HIGHEST


def dot(a, b):
    return jnp.dot(a, b, precision=highest, preferred_element_type=jnp.float32)


def dot_nt(a, b):
    return lax.dot_general(
        a, b, (((1,), (1,)), ((), ())), precision=highest, preferred_element_type=jnp.float32
    )


def embedded(re, im):
    return jnp.concatenate(
        [jnp.concatenate([re, -im], axis=1), jnp.concatenate([im, re], axis=1)], axis=0
    )


def mixed(own, other, own_re, own_im, other_re, other_im):
    re = (own[0] * own_re - own[1] * own_im) + (other[0] * other_re - other[1] * other_im)
    im = (own[0] * own_im + own[1] * own_re) + (other[0] * other_im + other[1] * other_re)
    return re, im


def kernel(
    dims,
    x_ref, half_ref, low_ref, mid_ref, pair_in, bits_in, angle_ref,
    out_v,
    x_v, low_v, mid_v, angle_v, pair_ref, bits_ref,
    early_rx, early_y, early_t, late_y, late_t, late_z, late_rz, passing, stash,
    load_sem, ze_send, ze_recv, hop_sem, onward_sem, trade_send, trade_recv,
    zl_send, zl_recv, stash_sem, after_sem, near_sem, all_sem,
):
    groups, swaps, m_size, rows, low, early, lead, most, cuts, direct = dims
    late = rows - early
    part = m_size // swaps
    blocks = len(cuts) - 1
    grp = lax.axis_index("grp")
    me = lax.axis_index("swap")
    half = groups // 2
    quarter = groups // 4
    top = grp // half
    layer = grp // quarter
    partner = (grp + half) % groups

    def on(*layers):
        hit = layer == layers[0]
        for other in layers[1:]:
            hit = jnp.logical_or(hit, layer == other)
        return pl.when(hit)

    def tell(sem, to):
        pl.semaphore_signal(sem, inc=1, device_id={"grp": to}, device_id_type=MESH)

    def tell_peers(sem):
        for d in range(1, swaps):
            pl.semaphore_signal(
                sem, inc=1, device_id={"swap": lax.bitwise_xor(me, d)}, device_id_type=MESH
            )

    def remote(src, dst, send, recv, to):
        return pltpu.make_async_remote_copy(
            src_ref=src, dst_ref=dst, send_sem=send, recv_sem=recv,
            device_id={"grp": to}, device_id_type=MESH,
        )

    barrier = pltpu.get_barrier_semaphore()

    @on(2)
    def _():
        tell(barrier, grp - quarter)
        tell(barrier, grp - half)
        tell(barrier, grp + quarter)

    @on(0)
    def _():
        tell(barrier, grp + half)
        tell(barrier, grp + half + quarter)

    @on(1)
    def _():
        tell(barrier, grp + half)

    @on(3)
    def _():
        tell_peers(barrier)

    up = (grp + quarter) % groups
    first, second = pl.ds(0, lead), pl.ds(lead, most - lead)

    def raw_copy(at, sem):
        return remote(half_ref.at[:, at, 0], early_rx.at[:, at], ze_send, sem, partner)

    raw_most = raw_copy(pl.ds(0, most), ze_recv.at[0])
    raw_second = raw_copy(second, ze_recv.at[0])
    raw_last = raw_copy(pl.ds(most, m_size - most), ze_recv.at[1])
    all_raw = raw_copy(pl.ds(0, m_size), ze_recv.at[0])
    hop = remote(half_ref.at[:, first, 0], passing, ze_send, hop_sem, up)
    onward = remote(passing, early_rx.at[:, first], onward_sem, ze_recv.at[0], up)

    @on(0, 1, 2)
    def _():
        pl.semaphore_wait(barrier, 1)

    @on(3)
    def _():
        pl.semaphore_wait(barrier, swaps + 2)
        tell_peers(near_sem)

    on(0, 2, 3)(raw_most.start)
    on(0, 2, 3)(raw_last.start)
    on(1)(hop.start)
    loads = [
        pltpu.make_async_copy(src, dst, load_sem.at[i])
        for i, (src, dst) in enumerate(
            [(bits_in, bits_ref), (angle_ref, angle_v), (low_ref, low_v), (mid_ref, mid_v), (pair_in, pair_ref), (x_ref, x_v)]
        )
    ]
    for load in loads:
        load.start()

    @on(3)
    def _():
        pl.semaphore_wait(near_sem, swaps - 1)
        for back in range(1, 4):
            tell(all_sem, grp - back * quarter)

    def x_row(c, r):
        return x_v[pl.ds(c * m_size * rows + r, m_size, stride=rows), :]

    for load in loads:
        load.wait()
    theta = bits_ref[0].astype(jnp.float32) * angle_v[0:1, :]
    for j in range(1, angle_v.shape[0]):
        theta = theta + bits_ref[j].astype(jnp.float32) * angle_v[j : j + 1, :]
    cosine, sine = jnp.cos(theta), jnp.sin(theta)
    w = jnp.concatenate([low_v[0, 0], low_v[0, 1]], axis=0)
    for i in range(1, low_v.shape[0]):
        w = dot(embedded(low_v[i, 0], low_v[i, 1]), w)
    w_re, w_im = w[:low], w[low:]
    w = embedded(w_re * cosine - w_im * sine, w_re * sine + w_im * cosine)

    @on(0, 1, 2)
    def _():
        pl.semaphore_wait(all_sem, 1)

    on(1)(raw_second.start)
    on(1)(raw_last.start)
    mid_first = embedded(mid_v[0, 0], mid_v[0, 1])
    mid_second = embedded(mid_v[1, 0], mid_v[1, 1])

    def first_gates(pairs, y_ref):
        for i, (re, im) in enumerate(pairs):
            y = dot_nt(jnp.concatenate([re, im], axis=1), w)
            y = dot(mid_first, jnp.concatenate([y[:, :low], y[:, low:]], axis=0))
            y_ref[i, 0] = y[:m_size]
            y_ref[i, 1] = y[m_size:]

    def trade(y_ref, t_ref, recv):
        def copy(src_at, dst_at, to):
            return pltpu.make_async_remote_copy(
                src_ref=y_ref.at[:, :, src_at, :], dst_ref=t_ref.at[:, :, dst_at, :],
                send_sem=trade_send, recv_sem=recv,
                device_id={"swap": to}, device_id_type=MESH,
            )

        mine = pl.ds(pl.multiple_of(me * part, part), part)
        for d in range(1, swaps):
            to = lax.bitwise_xor(me, d)
            copy(pl.ds(pl.multiple_of(to * part, part), part), mine, to).start()
        t_ref[:, :, mine, :] = y_ref[:, :, mine, :]
        others = pl.ds(0, (swaps - 1) * part)
        copy(others, others, lax.bitwise_xor(me, 1)).wait()

    def last_gate(t_ref, i):
        z = dot(mid_second, jnp.concatenate([t_ref[i, 0], t_ref[i, 1]], axis=0))
        return z[:m_size], z[m_size:]

    own_re, own_im = pair_ref[0, top, top], pair_ref[1, top, top]
    other_re, other_im = pair_ref[0, top, 1 - top], pair_ref[1, top, 1 - top]

    first_gates([(x_row(0, r), x_row(1, r)) for r in range(early, rows)], late_y)

    @on(2)
    def _():
        hop.wait_recv()
        onward.start()

    trade(late_y, late_t, trade_recv.at[0])
    for i in range(late):
        z_re, z_im = last_gate(late_t, i)
        late_z[i, 0] = z_re
        late_z[i, 1] = z_im

    down = (grp + 3 * quarter) % groups
    finished, aside, after = [], [], []
    for k in range(blocks):
        at = pl.ds(cuts[k], cuts[k + 1] - cuts[k])
        src, dst = late_z.at[:, :, at, :], late_rz.at[:, :, at, :]
        finished.append(remote(src, dst, zl_send, zl_recv.at[k], partner))
        if k >= direct:
            by = stash.at[:, :, pl.ds(cuts[k] - cuts[direct], cuts[k + 1] - cuts[k]), :]
            aside.append(remote(src, by, zl_send, stash_sem.at[k - direct], down))
            after.append(remote(by, dst, after_sem, zl_recv.at[k], down))
    all_late = remote(late_z, late_rz, zl_send, zl_recv.at[0], partner)
    all_after = remote(stash, stash, after_sem, after_sem, down)

    @on(1)
    def _():
        for copy in finished:
            copy.start()

    @on(2)
    def _():
        for copy in finished:
            copy.start()
        for come, copy in zip(aside, after):
            come.wait_recv()
            copy.start()

    @on(3)
    def _():
        for copy in aside + finished[:direct]:
            copy.start()

    raw_most.wait_recv()

    @on(0)
    def _():
        for copy in finished:
            copy.start()

    raw_last.wait_recv()

    first_gates(
        [
            mixed(
                (x_row(0, r), x_row(1, r)), (early_rx[0, :, r, :], early_rx[1, :, r, :]),
                own_re, own_im, other_re, other_im,
            )
            for r in range(early)
        ],
        early_y,
    )
    trade(early_y, early_t, trade_recv.at[1])
    for r in range(early):
        for c, value in enumerate(last_gate(early_t, r)):
            out_v[pl.ds(c * m_size * rows + r, m_size, stride=rows), :] = value

    for k in range(blocks):
        if k == blocks - 1:
            all_raw.wait_send()
            all_late.wait_send()

            @on(2)
            def _():
                onward.wait_send()
                all_after.wait_send()

        finished[k].wait_recv()
        at = slice(cuts[k], cuts[k + 1])
        for i in range(late):
            pair = mixed(
                (late_z[i, 0, at], late_z[i, 1, at]), (late_rz[i, 0, at], late_rz[i, 1, at]),
                own_re, own_im, other_re, other_im,
            )
            for c in range(2):
                start = (c * m_size + cuts[k]) * rows + early + i
                out_v[pl.ds(start, cuts[k + 1] - cuts[k], stride=rows), :] = pair[c]


def local(groups, swaps, amplitudes, low_gates, mid_gates, pair_gate, slice_bits, phase_angles):
    _, _, _, a_size, b_size, q_size, rows, low = amplitudes.shape
    m_size = a_size * b_size * q_size
    early = rows // 2
    late = rows - early
    lead = m_size // 4
    most = m_size * 3 // 4
    cuts = [m_size * at // 8 for at in (0, 4, 5, 7, 8)]
    direct = 2
    flat = amplitudes.reshape(2 * m_size * rows, low)
    halves = amplitudes.reshape(2, m_size, 2, early, low)
    f32 = jnp.float32
    dma = pltpu.SemaphoreType.DMA
    regular = pltpu.SemaphoreType.REGULAR
    anywhere = pl.BlockSpec(memory_space=pl.ANY)
    in_hbm = [
        pltpu.with_memory_space_constraint(value, pltpu.HBM)
        for value in (flat, halves, low_gates, mid_gates, pair_gate, slice_bits, phase_angles)
    ]
    out = pl.pallas_call(
        functools.partial(kernel, (groups, swaps, m_size, rows, low, early, lead, most, cuts, direct)),
        out_shape=pltpu.VMEM(flat.shape, f32),
        in_specs=[anywhere] * 7,
        out_specs=pl.BlockSpec(memory_space=pltpu.VMEM),
        scratch_shapes=[
            pltpu.VMEM(flat.shape, f32),
            pltpu.VMEM(low_gates.shape, f32),
            pltpu.VMEM(mid_gates.shape, f32),
            pltpu.VMEM(phase_angles.shape, f32),
            pltpu.SMEM(pair_gate.shape, f32),
            pltpu.SMEM(slice_bits.shape, jnp.int32),
            pltpu.VMEM((2, m_size, early, low), f32),
        ]
        + [pltpu.VMEM((early, 2, m_size, low), f32)] * 2
        + [pltpu.VMEM((late, 2, m_size, low), f32)] * 4
        + [
            pltpu.VMEM((2, lead, early, low), f32),
            pltpu.VMEM((late, 2, m_size - cuts[direct], low), f32),
            dma((6,)), dma, dma((2,)), dma, dma, dma, dma((2,)),
            dma, dma((len(cuts) - 1,)), dma((len(cuts) - 1 - direct,)), dma, regular, regular,
        ],
        compiler_params=pltpu.CompilerParams(
            collective_id=0, has_side_effects=True, vmem_limit_bytes=24 << 20
        ),
        name="evolve",
    )(*in_hbm)
    return out.reshape(amplitudes.shape)


def solution(mesh):
    spec = P(None, "grp", "swap", None, None, None, None, None)
    return jax.shard_map(
        functools.partial(local, mesh.shape["grp"], mesh.shape["swap"]),
        mesh=mesh,
        in_specs=(spec, P(), P(), P(), P(), P()),
        out_specs=spec,
        check_vma=False,
    )
```

```python
import functools

import jax
import jax.numpy as jnp
from jax import lax
from jax.experimental import pallas as pl
from jax.experimental.pallas import tpu as pltpu
from jax.sharding import PartitionSpec as P

MESH = pl.DeviceIdType.MESH
highest = lax.Precision.HIGHEST


def dot(a, b):
    return jnp.dot(a, b, precision=highest, preferred_element_type=jnp.float32)


def dot_nt(a, b):
    return lax.dot_general(
        a, b, (((1,), (1,)), ((), ())), precision=highest, preferred_element_type=jnp.float32
    )


def embedded(re, im):
    return jnp.concatenate(
        [jnp.concatenate([re, -im], axis=1), jnp.concatenate([im, re], axis=1)], axis=0
    )


def mixed(own, other, own_re, own_im, other_re, other_im):
    re = (own[0] * own_re - own[1] * own_im) + (other[0] * other_re - other[1] * other_im)
    im = (own[0] * own_im + own[1] * own_re) + (other[0] * other_im + other[1] * other_re)
    return re, im


def kernel(
    dims,
    x_ref, half_ref, low_ref, mid_ref, pair_in, bits_in, angle_ref,
    out_v,
    x_v, low_v, mid_v, angle_v, pair_ref, bits_ref,
    early_rx, early_y, early_t, late_y, late_t, late_z, late_rz, ahead, passing, stash,
    load_sem, ze_send, ze_recv, hop_sem, onward_sem, trade_send, trade_recv,
    zl_send, zl_recv, stash_sem, after_sem, near_sem, all_sem,
):
    groups, swaps, m_size, rows, low, early, lead, most, cuts, direct = dims
    late = rows - early
    part = m_size // swaps
    blocks = len(cuts) - 1
    grp = lax.axis_index("grp")
    me = lax.axis_index("swap")
    half = groups // 2
    quarter = groups // 4
    top = grp // half
    layer = grp // quarter
    partner = (grp + half) % groups

    def on(*layers):
        hit = layer == layers[0]
        for other in layers[1:]:
            hit = jnp.logical_or(hit, layer == other)
        return pl.when(hit)

    def tell(sem, to):
        pl.semaphore_signal(sem, inc=1, device_id={"grp": to}, device_id_type=MESH)

    def tell_peers(sem):
        for d in range(1, swaps):
            pl.semaphore_signal(
                sem, inc=1, device_id={"swap": lax.bitwise_xor(me, d)}, device_id_type=MESH
            )

    def remote(src, dst, send, recv, to):
        return pltpu.make_async_remote_copy(
            src_ref=src, dst_ref=dst, send_sem=send, recv_sem=recv,
            device_id={"grp": to}, device_id_type=MESH,
        )

    barrier = pltpu.get_barrier_semaphore()

    @on(2)
    def _():
        tell(barrier, grp - quarter)
        tell(barrier, grp - half)
        tell(barrier, grp + quarter)

    @on(0)
    def _():
        tell(barrier, grp + half)
        tell(barrier, grp + half + quarter)

    @on(1)
    def _():
        tell(barrier, grp + half)

    @on(3)
    def _():
        tell_peers(barrier)

    up = (grp + quarter) % groups
    first, second = pl.ds(0, lead), pl.ds(lead, most - lead)

    def raw_copy(at, sem):
        return remote(half_ref.at[:, at, 0], early_rx.at[:, at], ze_send, sem, partner)

    raw_most = raw_copy(pl.ds(0, most), ze_recv.at[0])
    raw_second = raw_copy(second, ze_recv.at[0])
    raw_last = raw_copy(pl.ds(most, m_size - most), ze_recv.at[1])
    all_raw = raw_copy(pl.ds(0, m_size), ze_recv.at[0])
    hop = remote(ahead, passing, ze_send, hop_sem, up)
    fetch = pltpu.make_async_copy(half_ref.at[:, first, 0], ahead, load_sem.at[0])

    @on(1)
    def _():
        fetch.start()
        fetch.wait()
    onward = remote(passing, early_rx.at[:, first], onward_sem, ze_recv.at[0], up)

    @on(0, 1, 2)
    def _():
        pl.semaphore_wait(barrier, 1)

    @on(3)
    def _():
        pl.semaphore_wait(barrier, swaps + 2)
        tell_peers(near_sem)

    on(0, 2, 3)(raw_most.start)
    on(0, 2, 3)(raw_last.start)
    on(1)(hop.start)
    loads = [
        pltpu.make_async_copy(src, dst, sem)
        for src, dst, sem in (
            (bits_in, bits_ref, load_sem.at[0]), (angle_ref, angle_v, load_sem.at[1]),
            (low_ref, low_v, trade_send), (mid_ref, mid_v, zl_send),
            (pair_in, pair_ref, after_sem), (x_ref, x_v, onward_sem),
        )
    ]
    for load in loads:
        load.start()

    @on(3)
    def _():
        pl.semaphore_wait(near_sem, swaps - 1)
        for back in range(1, 4):
            tell(all_sem, grp - back * quarter)

    def x_row(c, r):
        return x_v[pl.ds(c * m_size * rows + r, m_size, stride=rows), :]

    for load in loads:
        load.wait()
    theta = bits_ref[0].astype(jnp.float32) * angle_v[0:1, :]
    for j in range(1, angle_v.shape[0]):
        theta = theta + bits_ref[j].astype(jnp.float32) * angle_v[j : j + 1, :]
    cosine, sine = jnp.cos(theta), jnp.sin(theta)
    w = jnp.concatenate([low_v[0, 0], low_v[0, 1]], axis=0)
    for i in range(1, low_v.shape[0]):
        w = dot(embedded(low_v[i, 0], low_v[i, 1]), w)
    w_re, w_im = w[:low], w[low:]
    w = embedded(w_re * cosine - w_im * sine, w_re * sine + w_im * cosine)

    @on(0, 1, 2)
    def _():
        pl.semaphore_wait(all_sem, 1)

    on(1)(raw_second.start)
    on(1)(raw_last.start)
    mid_first = embedded(mid_v[0, 0], mid_v[0, 1])
    mid_second = embedded(mid_v[1, 0], mid_v[1, 1])

    def first_gates(pairs, y_ref):
        for i, (re, im) in enumerate(pairs):
            y = dot_nt(jnp.concatenate([re, im], axis=1), w)
            y = dot(mid_first, jnp.concatenate([y[:, :low], y[:, low:]], axis=0))
            y_ref[i, 0] = y[:m_size]
            y_ref[i, 1] = y[m_size:]

    def trade(y_ref, t_ref, recv):
        def copy(src_at, dst_at, to):
            return pltpu.make_async_remote_copy(
                src_ref=y_ref.at[:, :, src_at, :], dst_ref=t_ref.at[:, :, dst_at, :],
                send_sem=trade_send, recv_sem=recv,
                device_id={"swap": to}, device_id_type=MESH,
            )

        mine = pl.ds(pl.multiple_of(me * part, part), part)
        for d in range(1, swaps):
            to = lax.bitwise_xor(me, d)
            copy(pl.ds(pl.multiple_of(to * part, part), part), mine, to).start()
        t_ref[:, :, mine, :] = y_ref[:, :, mine, :]
        others = pl.ds(0, (swaps - 1) * part)
        copy(others, others, lax.bitwise_xor(me, 1)).wait()

    def last_gate(t_ref, i):
        z = dot(mid_second, jnp.concatenate([t_ref[i, 0], t_ref[i, 1]], axis=0))
        return z[:m_size], z[m_size:]

    own_re, own_im = pair_ref[0, top, top], pair_ref[1, top, top]
    other_re, other_im = pair_ref[0, top, 1 - top], pair_ref[1, top, 1 - top]

    first_gates([(x_row(0, r), x_row(1, r)) for r in range(early, rows)], late_y)

    @on(2)
    def _():
        hop.wait_recv()
        onward.start()

    trade(late_y, late_t, trade_recv.at[0])
    for i in range(late):
        z_re, z_im = last_gate(late_t, i)
        late_z[i, 0] = z_re
        late_z[i, 1] = z_im

    down = (grp + 3 * quarter) % groups
    finished, aside, after = [], [], []
    for k in range(blocks):
        at = pl.ds(cuts[k], cuts[k + 1] - cuts[k])
        src, dst = late_z.at[:, :, at, :], late_rz.at[:, :, at, :]
        finished.append(remote(src, dst, zl_send, zl_recv.at[k], partner))
        if k >= direct:
            by = stash.at[:, :, pl.ds(cuts[k] - cuts[direct], cuts[k + 1] - cuts[k]), :]
            aside.append(remote(src, by, zl_send, stash_sem, down))
            after.append(remote(by, dst, after_sem, zl_recv.at[k], down))
    all_late = remote(late_z, late_rz, zl_send, zl_recv.at[0], partner)
    all_aside = remote(stash, stash, zl_send, stash_sem, down)
    all_after = remote(stash, stash, after_sem, after_sem, down)

    @on(1)
    def _():
        for copy in finished:
            copy.start()

    @on(2)
    def _():
        for copy in finished:
            copy.start()
        all_aside.wait_recv()
        for copy in after:
            copy.start()

    @on(3)
    def _():
        for copy in aside + finished[:direct]:
            copy.start()

    raw_most.wait_recv()

    @on(0)
    def _():
        for copy in finished:
            copy.start()

    raw_last.wait_recv()

    first_gates(
        [
            mixed(
                (x_row(0, r), x_row(1, r)), (early_rx[0, :, r, :], early_rx[1, :, r, :]),
                own_re, own_im, other_re, other_im,
            )
            for r in range(early)
        ],
        early_y,
    )
    trade(early_y, early_t, trade_recv.at[1])
    for r in range(early):
        for c, value in enumerate(last_gate(early_t, r)):
            out_v[pl.ds(c * m_size * rows + r, m_size, stride=rows), :] = value

    for k in range(blocks):
        if k == blocks - 1:
            all_raw.wait_send()
            all_late.wait_send()

            @on(2)
            def _():
                onward.wait_send()
                all_after.wait_send()

        finished[k].wait_recv()
        at = slice(cuts[k], cuts[k + 1])
        for i in range(late):
            pair = mixed(
                (late_z[i, 0, at], late_z[i, 1, at]), (late_rz[i, 0, at], late_rz[i, 1, at]),
                own_re, own_im, other_re, other_im,
            )
            for c in range(2):
                start = (c * m_size + cuts[k]) * rows + early + i
                out_v[pl.ds(start, cuts[k + 1] - cuts[k], stride=rows), :] = pair[c]


def local(groups, swaps, amplitudes, low_gates, mid_gates, pair_gate, slice_bits, phase_angles):
    _, _, _, a_size, b_size, q_size, rows, low = amplitudes.shape
    m_size = a_size * b_size * q_size
    early = rows // 2
    late = rows - early
    lead = m_size // 4
    most = m_size * 3 // 4
    cuts = [m_size * at // 8 for at in (0, 5, 7, 8)]
    direct = 1
    flat = amplitudes.reshape(2 * m_size * rows, low)
    halves = amplitudes.reshape(2, m_size, 2, early, low)
    f32 = jnp.float32
    dma = pltpu.SemaphoreType.DMA
    regular = pltpu.SemaphoreType.REGULAR
    anywhere = pl.BlockSpec(memory_space=pl.ANY)
    in_hbm = [
        pltpu.with_memory_space_constraint(value, pltpu.HBM)
        for value in (flat, halves, low_gates, mid_gates, pair_gate, slice_bits, phase_angles)
    ]
    out = pl.pallas_call(
        functools.partial(kernel, (groups, swaps, m_size, rows, low, early, lead, most, cuts, direct)),
        out_shape=pltpu.VMEM(flat.shape, f32),
        in_specs=[anywhere] * 7,
        out_specs=pl.BlockSpec(memory_space=pltpu.VMEM),
        scratch_shapes=[
            pltpu.VMEM(flat.shape, f32),
            pltpu.VMEM(low_gates.shape, f32),
            pltpu.VMEM(mid_gates.shape, f32),
            pltpu.VMEM(phase_angles.shape, f32),
            pltpu.SMEM(pair_gate.shape, f32),
            pltpu.SMEM(slice_bits.shape, jnp.int32),
            pltpu.VMEM((2, m_size, early, low), f32),
        ]
        + [pltpu.VMEM((early, 2, m_size, low), f32)] * 2
        + [pltpu.VMEM((late, 2, m_size, low), f32)] * 4
        + [
            pltpu.VMEM((2, lead, early, low), f32),
            pltpu.VMEM((2, lead, early, low), f32),
            pltpu.VMEM((late, 2, m_size - cuts[direct], low), f32),
            dma((2,)), dma, dma((2,)), dma, dma, dma, dma((2,)),
            dma, dma((len(cuts) - 1,)), dma, dma, regular, regular,
        ],
        compiler_params=pltpu.CompilerParams(
            collective_id=0, has_side_effects=True, vmem_limit_bytes=24 << 20
        ),
        name="evolve",
    )(*in_hbm)
    return out.reshape(amplitudes.shape)


def solution(mesh):
    spec = P(None, "grp", "swap", None, None, None, None, None)
    return jax.shard_map(
        functools.partial(local, mesh.shape["grp"], mesh.shape["swap"]),
        mesh=mesh,
        in_specs=(spec, P(), P(), P(), P(), P()),
        out_specs=spec,
        check_vma=False,
    )
```
